128 devices in a mesh: clip: 4 (over y_hi, core), ctx: 32 (over x, z, y_lo).
Axes of the slice: x: 4, y: 4 (y_hi: 2, y_lo: 2; y = y_hi * 2 + y_lo), z: 4, core: 2. Of those that a mesh axis runs over, the one named last changes fastest.
Arguments:
- queries: bfloat16 [16384, 4096], P(('clip', 'ctx')), parts along dimension 0, may hold values from -48 to 48
- key_rows: bfloat16 [16384, 4096], P(('clip', 'ctx')), parts along dimension 0, may hold values from -48 to 48
- values: bfloat16 [16384, 4096], P(('clip', 'ctx')), parts along dimension 0, may hold values from -6 to 6
- tangent_queries: bfloat16 [16384, 4096], P(('clip', 'ctx')), parts along dimension 0, may hold values from -6 to 6
- tangent_keys: bfloat16 [16384, 4096], P(('clip', 'ctx')), parts along dimension 0, may hold values from -6 to 6
- tangent_values: bfloat16 [16384, 4096], P(('clip', 'ctx')), parts along dimension 0, may hold values from -6 to 6
Outputs:
- attended: bfloat16 [16384, 4096], P(('clip', 'ctx')), parts along dimension 0
- tangent_output: bfloat16 [16384, 4096], P(('clip', 'ctx')), parts along dimension 0
The draws below stay inside these ranges and needn't reach their ends.
There are 4 independent parts, one for each index of `clip`. The reference program is written for one: setup_inputs(seed, part) draws one part's arguments, and reference() takes and returns one part's arrays. A program takes and returns all parts, laid end to end along the dimension named above; each array names one. Nothing has to cross between parts.
All inputs are finite; a program needn't handle non-finite values.
Results may differ from the reference program's by a relative error of at most 0.012.
Values may be sent and summed in bfloat16 or wider, within the bound.
No kernel may reach another device: no remote copies, remote signals or barrier semaphores. Data moves between devices by JAX's collectives and lax.ppermute only.
A program may use at most 64 MiB of HBM per device.

```python
import jax
import jax.numpy as jnp
from jax import lax

HD = 128
HEADS = 32
TOKENS = 4096


def draw_queries(key, part):
    drawn = jnp.clip(jax.random.normal(jax.random.fold_in(key, 1), (TOKENS, HEADS * HD), jnp.float32), -6.0, 6.0)
    return drawn.astype(jnp.bfloat16)


def draw_key_rows(key, part):
    drawn = jnp.clip(jax.random.normal(jax.random.fold_in(key, 2), (TOKENS, HEADS * HD), jnp.float32), -6.0, 6.0)
    return drawn.astype(jnp.bfloat16)


def steps_of(stream_key, shape, cuts, low, high):
    def one(dim, parts):
        draws = jax.random.uniform(jax.random.fold_in(jax.random.fold_in(stream_key, 6), dim), (parts,), jnp.float32, low / len(cuts), high / len(cuts))
        return jnp.repeat(jnp.exp(draws), shape[dim] // parts).reshape((-1,) + (1,) * (len(shape) - dim - 1))

    level = one(*cuts[0])
    for cut in cuts[1:]:
        level = level * one(*cut)
    return level


def scatter_about(stream_key, extent, width, limit, pieces=(), held_as=jnp.bfloat16):
    factor_of = steps_of(stream_key, extent, pieces, -0.22, 0.18) if pieces else 1.0
    entries = jax.random.normal(stream_key, extent, jnp.float32) * width * factor_of
    return jnp.minimum(jnp.maximum(entries, -limit), limit).astype(held_as)


def setup_inputs(seed: int = 0, part: int = 0) -> dict:
    keys = jax.random.split(jax.random.key(seed), 7)
    own_keys = jax.random.split(jax.random.fold_in(keys[6], part), 7)
    queries = draw_queries(jax.random.fold_in(jax.random.fold_in(keys[6], part), 71), part)
    key_rows = draw_key_rows(jax.random.fold_in(jax.random.fold_in(keys[6], part), 71), part)
    values = scatter_about(own_keys[2], (TOKENS, HEADS * HD), 1.0, 6.0, ((0, 32),))
    tangent_queries = scatter_about(own_keys[3], (TOKENS, HEADS * HD), 1.0, 6.0, ((0, 32),))
    tangent_keys = scatter_about(own_keys[4], (TOKENS, HEADS * HD), 1.0, 6.0, ((0, 32),))
    tangent_values = scatter_about(own_keys[5], (TOKENS, HEADS * HD), 1.0, 6.0, ((0, 32),))
    return dict(queries=queries, key_rows=key_rows, values=values, tangent_queries=tangent_queries, tangent_keys=tangent_keys, tangent_values=tangent_values)


def reference(queries, key_rows, values, tangent_queries, tangent_keys, tangent_values):
    scale = HD ** -0.5

    def by_heads(array):
        return jnp.transpose(array.reshape(TOKENS, HEADS, HD), (1, 0, 2))

    def side_by_side(array):
        return jnp.transpose(array, (1, 0, 2)).reshape(TOKENS, HEADS * HD)

    def one_head(group):
        query_head, key_head, value_head, tquery_head, tkey_head, tvalue_head = group
        scores = jnp.dot(query_head, key_head.T, preferred_element_type=jnp.float32) * scale
        probs = jax.nn.softmax(scores, axis=-1)
        dscores = (jnp.dot(tquery_head, key_head.T, preferred_element_type=jnp.float32)
                   + jnp.dot(query_head, tkey_head.T, preferred_element_type=jnp.float32)) * scale
        weighted = probs * dscores
        correction = jnp.sum(weighted, axis=-1, keepdims=True)
        prob_half = probs.astype(jnp.bfloat16)
        weight_half = weighted.astype(jnp.bfloat16)
        primal = jnp.dot(prob_half, value_head, preferred_element_type=jnp.float32)
        tangent = (jnp.dot(weight_half, value_head, preferred_element_type=jnp.float32)
                   + jnp.dot(prob_half, tvalue_head, preferred_element_type=jnp.float32)
                   - correction * primal)
        return primal.astype(jnp.bfloat16), tangent.astype(jnp.bfloat16)

    results = lax.map(one_head, tuple(by_heads(array) for array in (queries, key_rows, values, tangent_queries, tangent_keys, tangent_values)))
    return (side_by_side(results[0]), side_by_side(results[1]))
```

```python
import functools

import jax
import jax.numpy as jnp
from jax import lax
from jax.experimental import pallas as pl
from jax.experimental.pallas import tpu as pltpu
from jax.sharding import PartitionSpec as P

HD = 128
PAIR = 2 * HD
SCALE = HD**-0.5
TO_LOG2 = 1.4426950408889634 * SCALE
CONTRACT_LAST = (((1,), (1,)), ((), ()))
BF16 = jnp.bfloat16
F32 = jnp.float32
VMEM_BYTES = 56 * 2**20


def dot_last(a, b):
    return lax.dot_general(a, b, CONTRACT_LAST, preferred_element_type=F32)


def dot(a, b):
    return jnp.dot(a, b, preferred_element_type=F32)


def pack_kernel(pairs, heads, *refs):
    ins, out = refs[:-1], refs[-1]
    row = 0
    for which, (start, count) in enumerate(pairs):
        left, right = ins[2 * which], ins[2 * which + 1]
        for h in range(heads):
            cols = slice(h * HD, (h + 1) * HD)
            out[h, row : row + count, :HD] = left[start : start + count, cols]
            out[h, row : row + count, HD:] = right[start : start + count, cols]
        row += count


def pack(arrays, pairs, heads=4):
    tokens, width = arrays[0].shape
    groups = width // HD
    rows = sum(count for _, count in pairs)
    return pl.pallas_call(
        functools.partial(pack_kernel, pairs, heads),
        grid=(groups // heads,),
        in_specs=[pl.BlockSpec((tokens, heads * HD), lambda i: (0, i))] * len(arrays),
        out_specs=pl.BlockSpec((heads, rows, PAIR), lambda i: (i, 0, 0)),
        out_shape=jax.ShapeDtypeStruct((groups, rows, PAIR), BF16),
        cost_estimate=pl.CostEstimate(
            flops=0, bytes_accessed=4 * groups * rows * PAIR, transcendentals=0
        ),
        name="pack",
    )(*arrays)


def unpack_kernel(heads, count, *refs):
    parts, (left, right) = refs[:count], refs[count:]
    row = 0
    for part in parts:
        rows = part.shape[1]
        for h in range(heads):
            cols = slice(h * HD, (h + 1) * HD)
            left[row : row + rows, cols] = part[h, :, :HD]
            right[row : row + rows, cols] = part[h, :, HD:]
        row += rows


def unpack(parts, heads=4):
    groups = parts[0].shape[0]
    tokens = sum(part.shape[1] for part in parts)
    out = jax.ShapeDtypeStruct((tokens, groups * HD), BF16)
    return pl.pallas_call(
        functools.partial(unpack_kernel, heads, len(parts)),
        grid=(groups // heads,),
        in_specs=[
            pl.BlockSpec((heads, part.shape[1], PAIR), lambda i: (i, 0, 0)) for part in parts
        ],
        out_specs=[pl.BlockSpec((tokens, heads * HD), lambda i: (0, i))] * 2,
        out_shape=[out, out],
        cost_estimate=pl.CostEstimate(
            flops=0, bytes_accessed=8 * tokens * groups * HD, transcendentals=0
        ),
        name="unpack",
    )(*parts)


def attend(tqq, keys, vals, twice, ones, scores, chunk, before):
    block, total = tqq.shape[0], keys.shape[0]
    scaled = tqq[:, HD:].astype(F32) * TO_LOG2
    high = scaled.astype(BF16)
    low = (scaled - high.astype(F32)).astype(BF16)
    query = jnp.concatenate([high, low], axis=1)
    top = jnp.full((block, HD), -jnp.inf, F32) if before is None else before[0]
    for start in range(0, total, chunk):
        part = dot_last(query, twice[start : start + chunk, :])
        scores[:, start : start + chunk] = part
        for c in range(0, chunk, HD):
            top = jnp.maximum(top, part[:, c : c + HD])
    top = jnp.broadcast_to(jnp.max(top, axis=1, keepdims=True), (block, HD))
    if before is None:
        norm = jnp.zeros((block, HD), F32)
        both = jnp.zeros((block, PAIR), F32)
        tangent = jnp.zeros((block, PAIR), F32)
    else:
        decay = jnp.exp2(before[0] - top)
        wide = jnp.concatenate([decay, decay], axis=1)
        norm, both, tangent = before[1] * decay, before[2] * wide, before[3] * wide
    shift = top[:, :1]
    for start in range(0, total, chunk):
        rows = slice(start, start + chunk)
        raised = jnp.exp2(scores[:, rows] - shift)
        for c in range(0, chunk, HD):
            norm = norm + raised[:, c : c + HD]
        weighted = (raised * dot_last(tqq, keys[rows, :])).astype(BF16)
        both = both + dot(raised.astype(BF16), vals[rows, :])
        tangent = tangent + dot(weighted, ones[rows, :])
    return top, norm, both, tangent


def prepare(kv_ref, twice, ones, keys, vals):
    @pl.when(pl.program_id(0) == 0)
    def _():
        total = keys.shape[0]
        rows = kv_ref.shape[1] // 2
        both = kv_ref[:, :rows, :].reshape(total, PAIR)
        keys[...] = both
        twice[:, :HD] = both[:, :HD]
        twice[:, HD:] = both[:, :HD]
        both = kv_ref[:, rows:, :].reshape(total, PAIR)
        vals[...] = both
        ones[:, :HD] = both[:, :HD]
        ones[:, HD:] = jnp.ones((total, HD), BF16)


def first_kernel(chunk, q_ref, kv_ref, *refs):
    (top, norm, both, tangent), (scores, twice, ones, keys, vals) = refs[:4], refs[4:]
    prepare(kv_ref, twice, ones, keys, vals)
    tqq = q_ref[...].reshape(scores.shape[0], PAIR)
    top[...], norm[...], both[...], tangent[...] = attend(
        tqq, keys, vals, twice, ones, scores, chunk, None
    )


def last_kernel(chunk, q_ref, kv_ref, top, norm, both, tangent, out, scores, twice, ones, keys, vals):
    prepare(kv_ref, twice, ones, keys, vals)
    tqq = q_ref[...].reshape(scores.shape[0], PAIR)
    before = (top[...], norm[...], both[...], tangent[...])
    _, total, pair, weighted = attend(tqq, keys, vals, twice, ones, scores, chunk, before)
    share = 1.0 / jnp.sum(total, axis=1, keepdims=True)
    primal = pair[:, :HD] * share
    scaled = weighted * (share * SCALE)
    moved = scaled[:, :HD] + pair[:, HD:] * share - scaled[:, HD:] * primal
    out[:, :, :HD] = primal.astype(BF16).reshape(out.shape[0], out.shape[1], HD)
    out[:, :, HD:] = moved.astype(BF16).reshape(out.shape[0], out.shape[1], HD)


def cost(queries, keys):
    return pl.CostEstimate(
        flops=16 * queries * keys * HD, bytes_accessed=8 * queries * PAIR, transcendentals=queries * keys
    )


def call(kernel, name, received, kv, kv_rows, kv_at, q_at, q_rows, state, first_block, chunk):
    groups = received.shape[0]
    rows = 16
    block = groups * rows
    steps = q_rows // rows
    total = groups * kv_rows
    state_specs = [
        pl.BlockSpec((block, width), lambda i: (i + first_block, 0))
        for width in (HD, HD, PAIR, PAIR)
    ]
    if state is None:
        out_specs = state_specs
        out_shape = [
            jax.ShapeDtypeStruct((steps * block, width), F32) for width in (HD, HD, PAIR, PAIR)
        ]
        state, in_state = (), []
    else:
        out_specs = pl.BlockSpec((groups, rows, PAIR), lambda i: (0, i, 0))
        out_shape = jax.ShapeDtypeStruct((groups, q_rows, PAIR), BF16)
        in_state = state_specs
    return pl.pallas_call(
        functools.partial(kernel, chunk),
        grid=(steps,),
        in_specs=[
            pl.BlockSpec((groups, rows, PAIR), lambda i: (0, i + q_at // rows, 0)),
            pl.BlockSpec((groups, 2 * kv_rows, PAIR), lambda i: (0, kv_at // (2 * kv_rows), 0)),
            *in_state,
        ],
        out_specs=out_specs,
        out_shape=out_shape,
        scratch_shapes=[
            pltpu.VMEM((block, total), F32),
            pltpu.VMEM((total, PAIR), BF16),
            pltpu.VMEM((total, PAIR), BF16),
            pltpu.VMEM((total, PAIR), BF16),
            pltpu.VMEM((total, PAIR), BF16),
        ],
        compiler_params=pltpu.CompilerParams(vmem_limit_bytes=VMEM_BYTES),
        cost_estimate=cost(steps * block, total),
        name=name,
    )(received, kv, *state)


def exchange(array):
    return lax.all_to_all(array, "ctx", split_axis=0, concat_axis=0, tiled=True)


def body(queries, key_rows, values, tangent_queries, tangent_keys, tangent_values):
    tokens = queries.shape[0]
    half = tokens // 2
    kv = (key_rows, tangent_keys, values, tangent_values)
    one = exchange(
        pack((tangent_queries, queries, *kv), ((0, tokens), (0, half), (0, half)))
    )
    two = exchange(pack(kv, ((half, half), (half, half))))
    state = call(first_kernel, "first", one, one, half, tokens, 0, tokens, None, 0, 512)
    outs = []
    for part in range(2):
        q_rows = tokens // 2
        outs.append(
            exchange(
                call(
                    last_kernel,
                    f"last_{part}",
                    one,
                    two,
                    half,
                    0,
                    part * q_rows,
                    q_rows,
                    state,
                    part * q_rows // 16,
                    512,
                )
            )
        )
    return tuple(unpack(outs))


def solution(mesh):
    split = P(("clip", "ctx"), None)
    return jax.shard_map(
        body, mesh=mesh, in_specs=(split,) * 6, out_specs=(split, split), check_vma=False
    )
```

```python
import functools

import jax
import jax.numpy as jnp
from jax import lax
from jax.experimental import pallas as pl
from jax.experimental.pallas import tpu as pltpu
from jax.sharding import PartitionSpec as P

HD = 128
PAIR = 2 * HD
SCALE = HD**-0.5
TO_LOG2 = 1.4426950408889634 * SCALE
CONTRACT_LAST = (((1,), (1,)), ((), ()))
BF16 = jnp.bfloat16
F32 = jnp.float32
VMEM_BYTES = 62 * 2**20
WIDTHS = (HD, HD, PAIR, PAIR)

FIRST_ROWS = 64
OUT_ROWS = (128,)
LATER_NS = 0
SIDES = 2
SIDE_ROWS = 16
CHUNK = 512
VALUE_CHUNK = 512


def dot_last(a, b):
    return lax.dot_general(a, b, CONTRACT_LAST, preferred_element_type=F32)


def dot(a, b):
    return jnp.dot(a, b, preferred_element_type=F32)


def pack_kernel(pairs, per, late, *refs):
    count = 2 * len(pairs)
    if late:
        flag, refs = refs[0], refs[1:]

        @pl.when(flag[0] == 1)
        def _():
            pl.delay(late)

    ins, (out, held, arrived, left) = refs[:count], refs[count:]
    steps = held.shape[0] // per
    for g in range(steps):
        row = 0
        for which, (start, rows) in enumerate(pairs):
            for side in range(2):
                for h in range(g * per, (g + 1) * per):
                    pltpu.make_async_copy(
                        ins[2 * which + side].at[pl.ds(start, rows), pl.ds(h * HD, HD)],
                        held.at[h, pl.ds(row, rows), pl.ds(side * HD, HD)],
                        arrived.at[g],
                    ).start()
            row += rows
    for g in range(steps):
        group = pl.ds(g * per, per)
        pltpu.make_async_copy(out.at[group], held.at[group], arrived.at[g]).wait()
        pltpu.make_async_copy(held.at[group], out.at[group], left.at[g]).start()
    for g in range(steps):
        group = pl.ds(g * per, per)
        pltpu.make_async_copy(held.at[group], out.at[group], left.at[g]).wait()


def pack(arrays, pairs, later=None, per=8):
    groups = arrays[0].shape[1] // HD
    shape = (groups, sum(rows for _, rows in pairs), PAIR)
    anywhere = pl.BlockSpec(memory_space=pl.ANY)
    late = 0 if later is None else LATER_NS
    flags = [later] if late else []
    return pl.pallas_call(
        functools.partial(pack_kernel, pairs, per, late),
        in_specs=[pl.BlockSpec(memory_space=pltpu.SMEM)] * len(flags) + [anywhere] * len(arrays),
        out_specs=anywhere,
        out_shape=jax.ShapeDtypeStruct(shape, BF16),
        scratch_shapes=[
            pltpu.VMEM(shape, BF16),
            pltpu.SemaphoreType.DMA((groups // per,)),
            pltpu.SemaphoreType.DMA((groups // per,)),
        ],
        cost_estimate=pl.CostEstimate(
            flops=0, bytes_accessed=4 * shape[0] * shape[1] * PAIR, transcendentals=0
        ),
        name="pack",
    )(*flags, *arrays)


def unpack_kernel(per, count, *refs):
    parts, outs, held, arrived, left = (
        refs[:count],
        refs[count : count + 2],
        refs[count + 2 : 2 * count + 2],
        refs[-2],
        refs[-1],
    )
    steps = parts[0].shape[0] // per
    for g in range(steps):
        group = pl.ds(g * per, per)
        for p in range(count):
            pltpu.make_async_copy(
                parts[p].at[group], held[p].at[group], arrived.at[p, g]
            ).start()
    for g in range(steps):
        row = 0
        for p in range(count):
            group = pl.ds(g * per, per)
            rows = held[p].shape[1]
            pltpu.make_async_copy(parts[p].at[group], held[p].at[group], arrived.at[p, g]).wait()
            for h in range(g * per, (g + 1) * per):
                for side in range(2):
                    pltpu.make_async_copy(
                        held[p].at[h, :, pl.ds(side * HD, HD)],
                        outs[side].at[pl.ds(row, rows), pl.ds(h * HD, HD)],
                        left.at[p, g],
                    ).start()
            row += rows
    for g in range(steps):
        for p in range(count):
            group = pl.ds(g * per, per)
            pltpu.make_async_copy(held[p].at[group], parts[p].at[group], left.at[p, g]).wait()


def unpack(parts, per=8):
    groups = parts[0].shape[0]
    tokens = sum(part.shape[1] for part in parts)
    out = jax.ShapeDtypeStruct((tokens, groups * HD), BF16)
    anywhere = pl.BlockSpec(memory_space=pl.ANY)
    return pl.pallas_call(
        functools.partial(unpack_kernel, per, len(parts)),
        in_specs=[anywhere] * len(parts),
        out_specs=[anywhere] * 2,
        out_shape=[out, out],
        scratch_shapes=[pltpu.VMEM(part.shape, BF16) for part in parts]
        + [pltpu.SemaphoreType.DMA((len(parts), groups // per))] * 2,
        cost_estimate=pl.CostEstimate(
            flops=0, bytes_accessed=8 * tokens * groups * HD, transcendentals=0
        ),
        name="unpack",
    )(*parts)


def prepare(kv_ref, twice, ones, keys, vals):
    @pl.when(pl.program_id(0) == 0)
    def _():
        total = keys.shape[0]
        rows = kv_ref.shape[1] // 2
        both = kv_ref[:, :rows, :].reshape(total, PAIR)
        keys[...] = both
        twice[:, :HD] = both[:, :HD]
        twice[:, HD:] = both[:, :HD]
        both = kv_ref[:, rows:, :].reshape(total, PAIR)
        vals[...] = both
        ones[:, :HD] = both[:, :HD]
        ones[:, HD:] = jnp.ones((total, HD), BF16)


class Side:
    def __init__(self, tqq, before, store, held, keyed, chunk):
        scaled = tqq[:, HD:].astype(F32) * TO_LOG2
        high = scaled.astype(BF16)
        low = (scaled - high.astype(F32)).astype(BF16)
        self.tqq, self.query = tqq, jnp.concatenate([high, low], axis=1)
        self.before, self.store, self.chunk, self.block = before, store, chunk, tqq.shape[0]
        self.scores, self.probs, self.weights = held
        self.twice, self.ones, self.keys, self.vals = keyed
        if before is None:
            self.top = jnp.full((self.block, HD), -jnp.inf, F32)
        else:
            self.top = before[0][...]
        self.both = self.tangent = None

    def score(self, start):
        part = dot_last(self.query, self.twice[start : start + self.chunk, :])
        self.scores[:, start : start + self.chunk] = part
        for c in range(0, self.chunk, HD):
            self.top = jnp.maximum(self.top, part[:, c : c + HD])

    def peak(self):
        self.top = jnp.broadcast_to(jnp.max(self.top, axis=1, keepdims=True), (self.block, HD))
        if self.before is None:
            self.norm = jnp.zeros((self.block, HD), F32)
        else:
            self.decay = jnp.exp2(self.before[0][...] - self.top)
            self.norm = self.before[1][...] * self.decay

    def soften(self, start):
        rows = slice(start, start + self.chunk)
        raised = jnp.exp2(self.scores[:, rows] - self.top[:, :1])
        for c in range(0, self.chunk, HD):
            self.norm = self.norm + raised[:, c : c + HD]
        self.probs[:, rows] = raised.astype(BF16)
        self.weights[:, rows] = (raised * dot_last(self.tqq, self.keys[rows, :])).astype(BF16)

    def gather(self, start, size):
        rows = slice(start, start + size)
        both = dot(self.probs[:, rows], self.vals[rows, :])
        tangent = dot(self.weights[:, rows], self.ones[rows, :])
        self.both = both if self.both is None else self.both + both
        self.tangent = tangent if self.tangent is None else self.tangent + tangent

    def finish(self):
        if self.before is not None:
            wide = jnp.concatenate([self.decay, self.decay], axis=1)
            self.both = self.both + self.before[2][...] * wide
            self.tangent = self.tangent + self.before[3][...] * wide
        self.store(self.top, self.norm, self.both, self.tangent)


def attend(sides, total, chunk, value_chunk):
    for start in range(0, total, chunk):
        sides[0].score(start)
    previous = None
    for n, side in enumerate(sides):
        side.peak()
        done = 0
        for start in range(0, total, chunk):
            side.soften(start)
            if n + 1 < len(sides):
                sides[n + 1].score(start)
            while previous is not None and done + value_chunk <= start + chunk:
                previous.gather(done, value_chunk)
                done += value_chunk
        if previous is not None:
            if done < total:
                previous.gather(done, total - done)
            previous.finish()
        previous = side
    previous.gather(0, total)
    previous.finish()


def attention_kernel(count, resumes, ends, q_ref, kv_ref, *refs):
    refs = list(refs)
    take = lambda n: [refs.pop(0) for _ in range(n)]
    state = take(4) if resumes else None
    outs = take(1) if ends else take(4)
    twice, ones, keys, vals = take(4)
    prepare(kv_ref, twice, ones, keys, vals)
    groups, rows = q_ref.shape[0], q_ref.shape[1] // count
    block, total = groups * rows, keys.shape[0]
    sides = []
    for n in range(count):
        mine, tokens = slice(n * block, (n + 1) * block), slice(n * rows, (n + 1) * rows)

        def store(top, norm, both, tangent, mine=mine, tokens=tokens):
            if not ends:
                for ref, value in zip(outs, (top, norm, both, tangent)):
                    ref[mine, :] = value
                return
            share = 1.0 / jnp.sum(norm, axis=1, keepdims=True)
            primal = both[:, :HD] * share
            scaled = tangent * (share * SCALE)
            moved = scaled[:, :HD] + both[:, HD:] * share - scaled[:, HD:] * primal
            outs[0][:, tokens, :HD] = primal.astype(BF16).reshape(groups, rows, HD)
            outs[0][:, tokens, HD:] = moved.astype(BF16).reshape(groups, rows, HD)

        sides.append(
            Side(
                q_ref[:, tokens, :].reshape(block, PAIR),
                [ref.at[mine, :] for ref in state] if resumes else None,
                store,
                take(3),
                (twice, ones, keys, vals),
                CHUNK,
            )
        )
    attend(sides, total, CHUNK, VALUE_CHUNK)


def attention(name, queries, q_at, q_rows, kv, kv_at, kv_rows, state=None, state_at=0, ends=False):
    groups = queries.shape[0]
    rows = SIDES * SIDE_ROWS
    block, total, steps = groups * rows, groups * kv_rows, q_rows // rows
    if ends:
        out_specs = pl.BlockSpec((groups, rows, PAIR), lambda i: (0, i, 0))
        out_shape = jax.ShapeDtypeStruct((groups, q_rows, PAIR), BF16)
    else:
        out_specs = [pl.BlockSpec((block, width), lambda i: (i, 0)) for width in WIDTHS]
        out_shape = [jax.ShapeDtypeStruct((steps * block, width), F32) for width in WIDTHS]
    state_specs = [
        pl.BlockSpec((block, width), lambda i: (i + state_at // rows, 0)) for width in WIDTHS
    ]
    side = groups * SIDE_ROWS
    return pl.pallas_call(
        functools.partial(attention_kernel, SIDES, state is not None, ends),
        grid=(steps,),
        in_specs=[
            pl.BlockSpec((groups, rows, PAIR), lambda i: (0, i + q_at // rows, 0)),
            pl.BlockSpec((groups, 2 * kv_rows, PAIR), lambda i: (0, kv_at // (2 * kv_rows), 0)),
            *(state_specs if state is not None else ()),
        ],
        out_specs=out_specs,
        out_shape=out_shape,
        scratch_shapes=[pltpu.VMEM((total, PAIR), BF16)] * 4
        + [
            pltpu.VMEM((side, total), F32),
            pltpu.VMEM((side, total), BF16),
            pltpu.VMEM((side, total), BF16),
        ]
        * SIDES,
        compiler_params=pltpu.CompilerParams(vmem_limit_bytes=VMEM_BYTES),
        cost_estimate=pl.CostEstimate(
            flops=16 * steps * block * total * HD,
            bytes_accessed=8 * steps * block * PAIR,
            transcendentals=steps * block * total,
        ),
        name=name,
    )(queries, kv, *(state or ()))


def exchange(array):
    return lax.all_to_all(array, "ctx", split_axis=0, concat_axis=0, tiled=True)


def body(queries, key_rows, values, tangent_queries, tangent_keys, tangent_values):
    tokens = queries.shape[0]
    early, rest = FIRST_ROWS, tokens - FIRST_ROWS
    kv = (key_rows, tangent_keys, values, tangent_values)
    later = (lax.axis_index("clip") % 2).astype(jnp.int32).reshape(1)
    one = exchange(
        pack(
            (*kv, tangent_queries, queries), ((0, early), (0, early), (0, tokens)), later
        )
    )
    two = exchange(pack(kv, ((early, rest), (early, rest))))
    q_at = 2 * early
    state = attention("first", one, q_at, tokens, one, 0, early)
    outs, at = [], 0
    for n, rows in enumerate(OUT_ROWS):
        outs.append(
            exchange(
                attention(f"last_{n}", one, q_at + at, rows, two, 0, rest, state, at, True)
            )
        )
        at += rows
    return tuple(unpack(outs))


def solution(mesh):
    split = P(("clip", "ctx"), None)
    return jax.shard_map(
        body, mesh=mesh, in_specs=(split,) * 6, out_specs=(split, split), check_vma=False
    )
```

```python
import functools

import jax
import jax.numpy as jnp
from jax import lax
from jax.experimental import pallas as pl
from jax.experimental.pallas import tpu as pltpu
from jax.sharding import PartitionSpec as P

HD = 128
PAIR = 2 * HD
SCALE = HD**-0.5
TO_LOG2 = 1.4426950408889634 * SCALE
CONTRACT_LAST = (((1,), (1,)), ((), ()))
BF16 = jnp.bfloat16
F32 = jnp.float32
VMEM_BYTES = 62 * 2**20
WIDTHS = (HD, HD, PAIR, PAIR)

FIRST_ROWS = 64
AHEAD_ROWS = 48
OUT_ROWS = (128,)
LATER_NS = 25000
SIDES = 2
SIDE_ROWS = 16
CHUNK = 512
VALUE_CHUNK = 512


def dot_last(a, b):
    return lax.dot_general(a, b, CONTRACT_LAST, preferred_element_type=F32)


def dot(a, b):
    return jnp.dot(a, b, preferred_element_type=F32)


def pack_kernel(pairs, per, late, *refs):
    count = 2 * len(pairs)
    if late:
        pl.delay(late)
    ins, (out, held, arrived, left) = refs[:count], refs[count:]
    steps = held.shape[0] // per
    for g in range(steps):
        row = 0
        for which, (start, rows) in enumerate(pairs):
            for side in range(2):
                for h in range(g * per, (g + 1) * per):
                    pltpu.make_async_copy(
                        ins[2 * which + side].at[pl.ds(start, rows), pl.ds(h * HD, HD)],
                        held.at[h, pl.ds(row, rows), pl.ds(side * HD, HD)],
                        arrived.at[g],
                    ).start()
            row += rows
    for g in range(steps):
        group = pl.ds(g * per, per)
        pltpu.make_async_copy(out.at[group], held.at[group], arrived.at[g]).wait()
        pltpu.make_async_copy(held.at[group], out.at[group], left.at[g]).start()
    for g in range(steps):
        group = pl.ds(g * per, per)
        pltpu.make_async_copy(held.at[group], out.at[group], left.at[g]).wait()


def pack(arrays, pairs, late=0, per=8):
    groups = arrays[0].shape[1] // HD
    shape = (groups, sum(rows for _, rows in pairs), PAIR)
    anywhere = pl.BlockSpec(memory_space=pl.ANY)
    return pl.pallas_call(
        functools.partial(pack_kernel, pairs, per, late),
        in_specs=[anywhere] * len(arrays),
        out_specs=anywhere,
        out_shape=jax.ShapeDtypeStruct(shape, BF16),
        scratch_shapes=[
            pltpu.VMEM(shape, BF16),
            pltpu.SemaphoreType.DMA((groups // per,)),
            pltpu.SemaphoreType.DMA((groups // per,)),
        ],
        cost_estimate=pl.CostEstimate(
            flops=0, bytes_accessed=4 * shape[0] * shape[1] * PAIR, transcendentals=0
        ),
        name="pack",
    )(*arrays)


def unpack_kernel(per, count, *refs):
    parts, outs, held, arrived, left = (
        refs[:count],
        refs[count : count + 2],
        refs[count + 2 : 2 * count + 2],
        refs[-2],
        refs[-1],
    )
    steps = parts[0].shape[0] // per
    for g in range(steps):
        group = pl.ds(g * per, per)
        for p in range(count):
            pltpu.make_async_copy(
                parts[p].at[group], held[p].at[group], arrived.at[p, g]
            ).start()
    for g in range(steps):
        row = 0
        for p in range(count):
            group = pl.ds(g * per, per)
            rows = held[p].shape[1]
            pltpu.make_async_copy(parts[p].at[group], held[p].at[group], arrived.at[p, g]).wait()
            for h in range(g * per, (g + 1) * per):
                for side in range(2):
                    pltpu.make_async_copy(
                        held[p].at[h, :, pl.ds(side * HD, HD)],
                        outs[side].at[pl.ds(row, rows), pl.ds(h * HD, HD)],
                        left.at[p, g],
                    ).start()
            row += rows
    for g in range(steps):
        for p in range(count):
            group = pl.ds(g * per, per)
            pltpu.make_async_copy(held[p].at[group], parts[p].at[group], left.at[p, g]).wait()


def unpack(parts, per=8):
    groups = parts[0].shape[0]
    tokens = sum(part.shape[1] for part in parts)
    out = jax.ShapeDtypeStruct((tokens, groups * HD), BF16)
    anywhere = pl.BlockSpec(memory_space=pl.ANY)
    return pl.pallas_call(
        functools.partial(unpack_kernel, per, len(parts)),
        in_specs=[anywhere] * len(parts),
        out_specs=[anywhere] * 2,
        out_shape=[out, out],
        scratch_shapes=[pltpu.VMEM(part.shape, BF16) for part in parts]
        + [pltpu.SemaphoreType.DMA((len(parts), groups // per))] * 2,
        cost_estimate=pl.CostEstimate(
            flops=0, bytes_accessed=8 * tokens * groups * HD, transcendentals=0
        ),
        name="unpack",
    )(*parts)


def prepare(kv_ref, ones, keys, vals):
    @pl.when(pl.program_id(0) == 0)
    def _():
        total = keys.shape[0]
        rows = kv_ref.shape[1] // 2
        keys[...] = kv_ref[:, :rows, :].reshape(total, PAIR)
        both = kv_ref[:, rows:, :].reshape(total, PAIR)
        vals[...] = both
        ones[:, :HD] = both[:, :HD]
        ones[:, HD:] = jnp.ones((total, HD), BF16)


class Side:
    def __init__(self, tqq, before, store, held, keyed, chunk):
        self.tqq, self.query = tqq, tqq[:, HD:]
        self.before, self.store, self.chunk, self.block = before, store, chunk, tqq.shape[0]
        self.scores, self.probs, self.weights = held
        self.ones, self.keys, self.vals = keyed
        if before is None:
            self.top = jnp.full((self.block, HD), -jnp.inf, F32)
        else:
            self.top = before[0][...]
        self.both = self.tangent = None

    def score(self, start):
        part = dot_last(self.query, self.keys[start : start + self.chunk, :HD])
        self.scores[:, start : start + self.chunk] = part
        for c in range(0, self.chunk, HD):
            self.top = jnp.maximum(self.top, part[:, c : c + HD])

    def peak(self):
        self.top = jnp.broadcast_to(jnp.max(self.top, axis=1, keepdims=True), (self.block, HD))
        if self.before is None:
            self.norm = jnp.zeros((self.block, HD), F32)
        else:
            self.decay = jnp.exp2((self.before[0][...] - self.top) * TO_LOG2)
            self.norm = self.before[1][...] * self.decay

    def soften(self, start):
        rows = slice(start, start + self.chunk)
        raised = jnp.exp2((self.scores[:, rows] - self.top[:, :1]) * TO_LOG2)
        for c in range(0, self.chunk, HD):
            self.norm = self.norm + raised[:, c : c + HD]
        self.probs[:, rows] = raised.astype(BF16)
        self.weights[:, rows] = (raised * dot_last(self.tqq, self.keys[rows, :])).astype(BF16)

    def gather(self, start, size):
        rows = slice(start, start + size)
        both = dot(self.probs[:, rows], self.vals[rows, :])
        tangent = dot(self.weights[:, rows], self.ones[rows, :])
        self.both = both if self.both is None else self.both + both
        self.tangent = tangent if self.tangent is None else self.tangent + tangent

    def finish(self):
        if self.before is not None:
            wide = jnp.concatenate([self.decay, self.decay], axis=1)
            self.both = self.both + self.before[2][...] * wide
            self.tangent = self.tangent + self.before[3][...] * wide
        self.store(self.top, self.norm, self.both, self.tangent)


def attend(sides, total, chunk, value_chunk):
    for start in range(0, total, chunk):
        sides[0].score(start)
    previous = None
    for n, side in enumerate(sides):
        side.peak()
        done = 0
        for start in range(0, total, chunk):
            side.soften(start)
            if n + 1 < len(sides):
                sides[n + 1].score(start)
            while previous is not None and done + value_chunk <= start + chunk:
                previous.gather(done, value_chunk)
                done += value_chunk
        if previous is not None:
            if done < total:
                previous.gather(done, total - done)
            previous.finish()
        previous = side
    previous.gather(0, total)
    previous.finish()


def attention_kernel(count, resumes, ends, q_ref, kv_ref, *refs):
    refs = list(refs)
    take = lambda n: [refs.pop(0) for _ in range(n)]
    state = take(4) if resumes else None
    outs = take(1) if ends else take(4)
    ones, keys, vals = take(3)
    prepare(kv_ref, ones, keys, vals)
    groups, rows = q_ref.shape[0], q_ref.shape[1] // count
    block, total = groups * rows, keys.shape[0]
    sides = []
    for n in range(count):
        mine, tokens = slice(n * block, (n + 1) * block), slice(n * rows, (n + 1) * rows)

        def store(top, norm, both, tangent, mine=mine, tokens=tokens):
            if not ends:
                for ref, value in zip(outs, (top, norm, both, tangent)):
                    ref[mine, :] = value
                return
            share = 1.0 / jnp.sum(norm, axis=1, keepdims=True)
            primal = both[:, :HD] * share
            scaled = tangent * (share * SCALE)
            moved = scaled[:, :HD] + both[:, HD:] * share - scaled[:, HD:] * primal
            outs[0][:, tokens, :HD] = primal.astype(BF16).reshape(groups, rows, HD)
            outs[0][:, tokens, HD:] = moved.astype(BF16).reshape(groups, rows, HD)

        sides.append(
            Side(
                q_ref[:, tokens, :].reshape(block, PAIR),
                [ref.at[mine, :] for ref in state] if resumes else None,
                store,
                take(3),
                (ones, keys, vals),
                CHUNK,
            )
        )
    attend(sides, total, CHUNK, VALUE_CHUNK)


def attention(name, queries, q_at, q_rows, kv, kv_at, kv_rows, state=None, state_at=0, ends=False):
    groups = queries.shape[0]
    rows = SIDES * SIDE_ROWS
    block, total, steps = groups * rows, groups * kv_rows, q_rows // rows
    if ends:
        out_specs = pl.BlockSpec((groups, rows, PAIR), lambda i: (0, i, 0))
        out_shape = jax.ShapeDtypeStruct((groups, q_rows, PAIR), BF16)
    else:
        out_specs = [pl.BlockSpec((block, width), lambda i: (i, 0)) for width in WIDTHS]
        out_shape = [jax.ShapeDtypeStruct((steps * block, width), F32) for width in WIDTHS]
    state_specs = [
        pl.BlockSpec((block, width), lambda i: (i + state_at // rows, 0)) for width in WIDTHS
    ]
    side = groups * SIDE_ROWS
    return pl.pallas_call(
        functools.partial(attention_kernel, SIDES, state is not None, ends),
        grid=(steps,),
        in_specs=[
            pl.BlockSpec((groups, rows, PAIR), lambda i: (0, i + q_at // rows, 0)),
            pl.BlockSpec((groups, 2 * kv_rows, PAIR), lambda i: (0, kv_at // (2 * kv_rows), 0)),
            *(state_specs if state is not None else ()),
        ],
        out_specs=out_specs,
        out_shape=out_shape,
        scratch_shapes=[pltpu.VMEM((total, PAIR), BF16)] * 3
        + [
            pltpu.VMEM((side, total), F32),
            pltpu.VMEM((side, total), BF16),
            pltpu.VMEM((side, total), BF16),
        ]
        * SIDES,
        compiler_params=pltpu.CompilerParams(vmem_limit_bytes=VMEM_BYTES),
        cost_estimate=pl.CostEstimate(
            flops=16 * steps * block * total * HD,
            bytes_accessed=8 * steps * block * PAIR,
            transcendentals=steps * block * total,
        ),
        name=name,
    )(queries, kv, *(state or ()))


def exchange(array):
    return lax.all_to_all(array, "ctx", split_axis=0, concat_axis=0, tiled=True)


def run(ahead, queries, key_rows, values, tangent_queries, tangent_keys, tangent_values):
    tokens = queries.shape[0]
    early = AHEAD_ROWS if ahead else FIRST_ROWS
    rest = tokens - early
    kv = (key_rows, tangent_keys, values, tangent_values)
    one = exchange(
        pack(
            (*kv, tangent_queries, queries),
            ((0, early), (0, early), (0, tokens)),
            0 if ahead else LATER_NS,
        )
    )
    two = pack(kv, ((early, rest), (early, rest)))
    q_at = 2 * early
    if ahead:
        state = attention("first", one, q_at, tokens, one, 0, early)
        two, *state = lax.optimization_barrier((two, *state))
        two = exchange(two)
    else:
        two = exchange(two)
        state = attention("first", one, q_at, tokens, one, 0, early)
    outs, at = [], 0
    for n, rows in enumerate(OUT_ROWS):
        outs.append(
            exchange(
                attention(f"last_{n}", one, q_at + at, rows, two, 0, rest, state, at, True)
            )
        )
        at += rows
    return tuple(unpack(outs))


def body(*arrays):
    ahead = lax.axis_index("clip") % 2 == 1
    return lax.cond(
        ahead, functools.partial(run, True), functools.partial(run, False), *arrays
    )


def solution(mesh):
    split = P(("clip", "ctx"), None)
    return jax.shard_map(
        body, mesh=mesh, in_specs=(split,) * 6, out_specs=(split, split), check_vma=False
    )
```

```python
import functools

import jax
import jax.numpy as jnp
from jax import lax
from jax.experimental import pallas as pl
from jax.experimental.pallas import tpu as pltpu
from jax.sharding import PartitionSpec as P

HD = 128
PAIR = 2 * HD
SCALE = HD**-0.5
TO_LOG2 = 1.4426950408889634 * SCALE
CONTRACT_LAST = (((1,), (1,)), ((), ()))
BF16 = jnp.bfloat16
F32 = jnp.float32
VMEM_BYTES = 62 * 2**20
WIDTHS = (HD, HD, PAIR, PAIR)

FIRST_ROWS = 64
AHEAD_ROWS = 48
OUT_ROWS = (128,)
LATER_NS = 24500
SIDES = 2
SIDE_ROWS = 16
CHUNK = 512
VALUE_CHUNK = 512


def dot_last(a, b):
    return lax.dot_general(a, b, CONTRACT_LAST, preferred_element_type=F32)


def dot(a, b):
    return jnp.dot(a, b, preferred_element_type=F32)


def pack_kernel(pairs, per, late, *refs):
    count = 2 * len(pairs)
    if late:
        pl.delay(late)
    ins, (out, held, arrived, left) = refs[:count], refs[count:]
    steps = held.shape[0] // per
    for g in range(steps):
        row = 0
        for which, (start, rows) in enumerate(pairs):
            for side in range(2):
                for h in range(g * per, (g + 1) * per):
                    pltpu.make_async_copy(
                        ins[2 * which + side].at[pl.ds(start, rows), pl.ds(h * HD, HD)],
                        held.at[h, pl.ds(row, rows), pl.ds(side * HD, HD)],
                        arrived.at[g],
                    ).start()
            row += rows
    for g in range(steps):
        group = pl.ds(g * per, per)
        pltpu.make_async_copy(out.at[group], held.at[group], arrived.at[g]).wait()
        pltpu.make_async_copy(held.at[group], out.at[group], left.at[g]).start()
    for g in range(steps):
        group = pl.ds(g * per, per)
        pltpu.make_async_copy(held.at[group], out.at[group], left.at[g]).wait()


def pack(arrays, pairs, late=0, per=8):
    groups = arrays[0].shape[1] // HD
    shape = (groups, sum(rows for _, rows in pairs), PAIR)
    anywhere = pl.BlockSpec(memory_space=pl.ANY)
    return pl.pallas_call(
        functools.partial(pack_kernel, pairs, per, late),
        in_specs=[anywhere] * len(arrays),
        out_specs=anywhere,
        out_shape=jax.ShapeDtypeStruct(shape, BF16),
        scratch_shapes=[
            pltpu.VMEM(shape, BF16),
            pltpu.SemaphoreType.DMA((groups // per,)),
            pltpu.SemaphoreType.DMA((groups // per,)),
        ],
        cost_estimate=pl.CostEstimate(
            flops=0, bytes_accessed=4 * shape[0] * shape[1] * PAIR, transcendentals=0
        ),
        name="pack",
    )(*arrays)


def unpack_kernel(per, count, *refs):
    parts, outs, held, arrived, left = (
        refs[:count],
        refs[count : count + 2],
        refs[count + 2 : 2 * count + 2],
        refs[-2],
        refs[-1],
    )
    steps = parts[0].shape[0] // per
    for g in range(steps):
        group = pl.ds(g * per, per)
        for p in range(count):
            pltpu.make_async_copy(
                parts[p].at[group], held[p].at[group], arrived.at[p, g]
            ).start()
    for g in range(steps):
        row = 0
        for p in range(count):
            group = pl.ds(g * per, per)
            rows = held[p].shape[1]
            pltpu.make_async_copy(parts[p].at[group], held[p].at[group], arrived.at[p, g]).wait()
            for h in range(g * per, (g + 1) * per):
                for side in range(2):
                    pltpu.make_async_copy(
                        held[p].at[h, :, pl.ds(side * HD, HD)],
                        outs[side].at[pl.ds(row, rows), pl.ds(h * HD, HD)],
                        left.at[p, g],
                    ).start()
            row += rows
    for g in range(steps):
        for p in range(count):
            group = pl.ds(g * per, per)
            pltpu.make_async_copy(held[p].at[group], parts[p].at[group], left.at[p, g]).wait()


def unpack(parts, per=8):
    groups = parts[0].shape[0]
    tokens = sum(part.shape[1] for part in parts)
    out = jax.ShapeDtypeStruct((tokens, groups * HD), BF16)
    anywhere = pl.BlockSpec(memory_space=pl.ANY)
    return pl.pallas_call(
        functools.partial(unpack_kernel, per, len(parts)),
        in_specs=[anywhere] * len(parts),
        out_specs=[anywhere] * 2,
        out_shape=[out, out],
        scratch_shapes=[pltpu.VMEM(part.shape, BF16) for part in parts]
        + [pltpu.SemaphoreType.DMA((len(parts), groups // per))] * 2,
        cost_estimate=pl.CostEstimate(
            flops=0, bytes_accessed=8 * tokens * groups * HD, transcendentals=0
        ),
        name="unpack",
    )(*parts)


def prepare(kv_ref, ones, keys, vals):
    @pl.when(pl.program_id(0) == 0)
    def _():
        total = keys.shape[0]
        rows = kv_ref.shape[1] // 2
        keys[...] = kv_ref[:, :rows, :].reshape(total, PAIR)
        both = kv_ref[:, rows:, :].reshape(total, PAIR)
        vals[...] = both
        ones[:, :HD] = both[:, :HD]
        ones[:, HD:] = jnp.ones((total, HD), BF16)


class Side:
    def __init__(self, tqq, before, store, held, keyed, chunk):
        self.tqq, self.query = tqq, tqq[:, HD:]
        self.before, self.store, self.chunk, self.block = before, store, chunk, tqq.shape[0]
        self.scores, self.probs, self.weights = held
        self.ones, self.keys, self.vals = keyed
        if before is None:
            self.top = jnp.full((self.block, HD), -jnp.inf, F32)
        else:
            self.top = before[0][...]
        self.both = self.tangent = None

    def score(self, start):
        part = dot_last(self.query, self.keys[start : start + self.chunk, :HD])
        self.scores[:, start : start + self.chunk] = part
        for c in range(0, self.chunk, HD):
            self.top = jnp.maximum(self.top, part[:, c : c + HD])

    def peak(self):
        self.top = jnp.broadcast_to(jnp.max(self.top, axis=1, keepdims=True), (self.block, HD))
        if self.before is None:
            self.norm = jnp.zeros((self.block, HD), F32)
        else:
            self.decay = jnp.exp2((self.before[0][...] - self.top) * TO_LOG2)
            self.norm = self.before[1][...] * self.decay

    def soften(self, start):
        rows = slice(start, start + self.chunk)
        raised = jnp.exp2((self.scores[:, rows] - self.top[:, :1]) * TO_LOG2)
        for c in range(0, self.chunk, HD):
            self.norm = self.norm + raised[:, c : c + HD]
        self.probs[:, rows] = raised.astype(BF16)
        self.weights[:, rows] = (raised * dot_last(self.tqq, self.keys[rows, :])).astype(BF16)

    def gather(self, start, size):
        rows = slice(start, start + size)
        both = dot(self.probs[:, rows], self.vals[rows, :])
        tangent = dot(self.weights[:, rows], self.ones[rows, :])
        self.both = both if self.both is None else self.both + both
        self.tangent = tangent if self.tangent is None else self.tangent + tangent

    def finish(self):
        if self.before is not None:
            wide = jnp.concatenate([self.decay, self.decay], axis=1)
            self.both = self.both + self.before[2][...] * wide
            self.tangent = self.tangent + self.before[3][...] * wide
        self.store(self.top, self.norm, self.both, self.tangent)


def attend(sides, total, chunk, value_chunk):
    for start in range(0, total, chunk):
        sides[0].score(start)
    previous = None
    for n, side in enumerate(sides):
        side.peak()
        done = 0
        for start in range(0, total, chunk):
            side.soften(start)
            if n + 1 < len(sides):
                sides[n + 1].score(start)
            while previous is not None and done + value_chunk <= start + chunk:
                previous.gather(done, value_chunk)
                done += value_chunk
        if previous is not None:
            if done < total:
                previous.gather(done, total - done)
            previous.finish()
        previous = side
    previous.gather(0, total)
    previous.finish()


def attention_kernel(count, resumes, ends, q_ref, kv_ref, *refs):
    refs = list(refs)
    take = lambda n: [refs.pop(0) for _ in range(n)]
    state = take(4) if resumes else None
    outs = take(1) if ends else take(4)
    ones, keys, vals = take(3)
    prepare(kv_ref, ones, keys, vals)
    groups, rows = q_ref.shape[0], q_ref.shape[1] // count
    block, total = groups * rows, keys.shape[0]
    sides = []
    for n in range(count):
        mine, tokens = slice(n * block, (n + 1) * block), slice(n * rows, (n + 1) * rows)

        def store(top, norm, both, tangent, mine=mine, tokens=tokens):
            if not ends:
                for ref, value in zip(outs, (top, norm, both, tangent)):
                    ref[mine, :] = value
                return
            share = 1.0 / jnp.sum(norm, axis=1, keepdims=True)
            primal = both[:, :HD] * share
            scaled = tangent * (share * SCALE)
            moved = scaled[:, :HD] + both[:, HD:] * share - scaled[:, HD:] * primal
            outs[0][:, tokens, :HD] = primal.astype(BF16).reshape(groups, rows, HD)
            outs[0][:, tokens, HD:] = moved.astype(BF16).reshape(groups, rows, HD)

        sides.append(
            Side(
                q_ref[:, tokens, :].reshape(block, PAIR),
                [ref.at[mine, :] for ref in state] if resumes else None,
                store,
                take(3),
                (ones, keys, vals),
                CHUNK,
            )
        )
    attend(sides, total, CHUNK, VALUE_CHUNK)


def attention(name, queries, q_at, q_rows, kv, kv_at, kv_rows, state=None, state_at=0, ends=False):
    groups = queries.shape[0]
    rows = SIDES * SIDE_ROWS
    block, total, steps = groups * rows, groups * kv_rows, q_rows // rows
    if ends:
        out_specs = pl.BlockSpec((groups, rows, PAIR), lambda i: (0, i, 0))
        out_shape = jax.ShapeDtypeStruct((groups, q_rows, PAIR), BF16)
    else:
        out_specs = [pl.BlockSpec((block, width), lambda i: (i, 0)) for width in WIDTHS]
        out_shape = [jax.ShapeDtypeStruct((steps * block, width), F32) for width in WIDTHS]
    state_specs = [
        pl.BlockSpec((block, width), lambda i: (i + state_at // rows, 0)) for width in WIDTHS
    ]
    side = groups * SIDE_ROWS
    return pl.pallas_call(
        functools.partial(attention_kernel, SIDES, state is not None, ends),
        grid=(steps,),
        in_specs=[
            pl.BlockSpec((groups, rows, PAIR), lambda i: (0, i + q_at // rows, 0)),
            pl.BlockSpec((groups, 2 * kv_rows, PAIR), lambda i: (0, kv_at // (2 * kv_rows), 0)),
            *(state_specs if state is not None else ()),
        ],
        out_specs=out_specs,
        out_shape=out_shape,
        scratch_shapes=[pltpu.VMEM((total, PAIR), BF16)] * 3
        + [
            pltpu.VMEM((side, total), F32),
            pltpu.VMEM((side, total), BF16),
            pltpu.VMEM((side, total), BF16),
        ]
        * SIDES,
        compiler_params=pltpu.CompilerParams(vmem_limit_bytes=VMEM_BYTES),
        cost_estimate=pl.CostEstimate(
            flops=16 * steps * block * total * HD,
            bytes_accessed=8 * steps * block * PAIR,
            transcendentals=steps * block * total,
        ),
        name=name,
    )(queries, kv, *(state or ()))


def exchange(array):
    return lax.all_to_all(array, "ctx", split_axis=0, concat_axis=0, tiled=True)


def run(ahead, queries, key_rows, values, tangent_queries, tangent_keys, tangent_values):
    tokens = queries.shape[0]
    early = AHEAD_ROWS if ahead else FIRST_ROWS
    rest = tokens - early
    kv = (key_rows, tangent_keys, values, tangent_values)
    one = exchange(
        pack(
            (*kv, tangent_queries, queries),
            ((0, early), (0, early), (0, tokens)),
            0 if ahead else LATER_NS,
        )
    )
    two = pack(kv, ((early, rest), (early, rest)))
    q_at = 2 * early
    if ahead:
        state = attention("first", one, q_at, tokens, one, 0, early)
        two, *state = lax.optimization_barrier((two, *state))
        two = exchange(two)
    else:
        two = exchange(two)
        state = attention("first", one, q_at, tokens, one, 0, early)
    outs, at = [], 0
    for n, rows in enumerate(OUT_ROWS):
        outs.append(
            exchange(
                attention(f"last_{n}", one, q_at + at, rows, two, 0, rest, state, at, True)
            )
        )
        at += rows
    return tuple(unpack(outs))


def body(*arrays):
    ahead = lax.axis_index("clip") % 2 == 1
    return lax.cond(
        ahead, functools.partial(run, True), functools.partial(run, False), *arrays
    )


def solution(mesh):
    split = P(("clip", "ctx"), None)
    return jax.shard_map(
        body, mesh=mesh, in_specs=(split,) * 6, out_specs=(split, split), check_vma=False
    )
```
